256 devices in a mesh: gy: 8 (over y, core), gx: 32 (over z, x).
Axes of the slice: x: 4, y: 4, z: 8, core: 2. Of those that a mesh axis runs over, the one named last changes fastest.
Arguments:
- ramp: int32 [32], replicated, may hold values from 0 to 7
- seed_mask: int32 [1024, 8192], P('gy', 'gx'), may hold values 0 or 1
- noise: float32 [2, 1024, 8192], P(None, 'gy', 'gx'), may hold values from -4 to 4
Outputs:
- filtered: float32 [32, 2, 1024, 8192], P(None, None, 'gy', 'gx')
- filter_matrix: float32 [32, 32], replicated
The draws below stay inside these ranges and needn't reach their ends.
All inputs are finite; a program needn't handle non-finite values. No bound on the sum of `seed_mask` on one device may be relied on, other than what follows from the above.
Results may differ from the reference program's by a relative error of at most 0.0045.
Values sent between devices are 32-bit elements; how exact they have to be, the bound alone decides.
A program may use at most 64 MiB of HBM per device.

```python
import jax
import jax.numpy as jnp
from jax import lax

SNAPS = 32
RATES = 8
NY = 1024
NX = 8192


def place_ends(values, key, smallest, high):
    dims = values.shape
    index_at = [jax.random.randint(jax.random.fold_in(key, axis), (), 0, dims[axis]) for axis in range(len(dims))]
    values = values.at[tuple(index_at)].set(smallest)
    longest = dims.index(max(dims))
    index_at[longest] = (index_at[longest] + 1) % dims[longest]
    return values.at[tuple(index_at)].set(high)


def block_levels(stream_key, extent, cuts, smallest, top_value):
    def one(position, blocks):
        draws = jax.random.uniform(jax.random.fold_in(jax.random.fold_in(stream_key, 6), position), (blocks,), jnp.float32, smallest / len(cuts), top_value / len(cuts))
        return jnp.repeat(jnp.exp(draws), extent[position] // blocks).reshape((-1,) + (1,) * (len(extent) - position - 1))

    level = one(*cuts[0])
    for cut in cuts[1:]:
        level = level * one(*cut)
    return level


def normal_values(stream_key, dims, spread, reach, pieces=(), kind=jnp.bfloat16):
    result = spread * jax.random.normal(stream_key, dims, jnp.float32)
    if pieces:
        result = result * block_levels(stream_key, dims, pieces, -0.22, 0.18)
    return jnp.clip(result, -reach, reach).astype(kind)


def setup_inputs(seed: int = 0) -> dict:
    keys = jax.random.split(jax.random.key(seed), 4)
    ramp = place_ends(jax.random.randint(keys[0], (SNAPS,), 0, RATES), jax.random.fold_in(keys[0], 1), 0, RATES - 1).astype(jnp.int32)
    seed_mask = place_ends((jax.random.randint(keys[1], (NY, NX), 0, 4) < 1).astype(jnp.int32), jax.random.fold_in(keys[1], 1), 0, 1)
    noise = normal_values(keys[2], (2, NY, NX), 1.0, 4.0, ((1, 8), (2, 32)), jnp.float32)
    return {"ramp": ramp, "seed_mask": seed_mask, "noise": noise}


def advance(padded, rate):
    center = padded[:, 1:-1, 1:-1]
    laplace = padded[:, :-2, 1:-1] + padded[:, 2:, 1:-1] + padded[:, 1:-1, :-2] + padded[:, 1:-1, 2:] - 4.0 * center
    u_now = center[0]
    v_now = center[1]
    react = u_now * v_now * v_now
    u_new = u_now + 0.2 * laplace[0] - react + rate * (1.0 - u_now)
    v_new = v_now + 0.1 * laplace[1] + react - (rate + 0.06) * v_now
    return jnp.stack([u_new, v_new])

def reference(ramp, seed_mask, noise):
    table = 0.01 + 0.008 * jnp.arange(RATES, dtype=jnp.float32)
    onehot = (ramp[:, None] == jnp.arange(RATES, dtype=jnp.int32)[None, :]).astype(jnp.float32)
    rates = jnp.sum(onehot * table[None, :], axis=1)
    row_pos = jnp.arange(NY, dtype=jnp.int32).astype(jnp.float32)
    amplitude = (0.5 + 1.5 * (row_pos + 0.5) / NY)[:, None]
    mask = seed_mask.astype(jnp.float32)
    u_start = 1.0 - 0.5 * mask + 0.1 * amplitude * noise[0]
    v_start = 0.25 * mask + 0.1 * amplitude * noise[1]
    state = jnp.stack([u_start, v_start])

    def one_step(current, rate):
        padded = jnp.pad(current, ((0, 0), (1, 1), (1, 1)), mode='wrap')
        fresh = advance(padded, rate)
        return (fresh, fresh)
    final, snaps = lax.scan(one_step, state, rates)
    average = jnp.mean(snaps, axis=0)
    centered = snaps - average[None]
    flat = centered.reshape(SNAPS, -1)
    gram = jnp.dot(flat.astype(jnp.float32), flat.T.astype(jnp.float32), precision=lax.Precision.HIGHEST, preferred_element_type=jnp.float32)
    shift_val = 0.01 * jnp.trace(gram) / SNAPS
    shifted = gram + shift_val * jnp.eye(SNAPS, dtype=jnp.float32)
    filter_matrix = jnp.linalg.solve(shifted, gram)
    filtered = jnp.dot(filter_matrix.T.astype(jnp.float32), flat.astype(jnp.float32), precision=lax.Precision.HIGHEST, preferred_element_type=jnp.float32)
    return (filtered.reshape(centered.shape), filter_matrix)
```

```python
import functools

import jax
import jax.numpy as jnp
from jax import lax
from jax.experimental import pallas as pl
from jax.experimental.pallas import tpu as pltpu
from jax.sharding import PartitionSpec as P

SNAPS = 32
ROWS = 128
COLS = 256
HALO = 32
PAD = 8
TOP = PAD + HALO
EXT = ROWS + 2 * TOP
BOTTOM = TOP + ROWS
LANES = 128
NGY = 8
NX = 4
NZ = 8
PLANE = NGY * NX
TILES = 2 * ROWS // 8
F32 = jnp.float32
BF16 = jnp.bfloat16
MESH = pl.DeviceIdType.MESH
HIGHEST = lax.Precision.HIGHEST


def iota(shape, dim):
    return lax.broadcasted_iota(jnp.int32, shape, dim)


def lane_roll(value, shift):
    return pltpu.roll(value, shift % LANES, 1)


def pack_first(u, v):
    half = u.shape[0] // 2
    quarter = iota((half, LANES), 1) // HALO
    out = jnp.where(quarter == 0, u[:half], lane_roll(v[:half], HALO))
    out = jnp.where(quarter == 2, lane_roll(u[half:], 2 * HALO), out)
    return jnp.where(quarter == 3, lane_roll(v[half:], 3 * HALO), out)


def pack_last(u, v):
    half = u.shape[0] // 2
    quarter = iota((half, LANES), 1) // HALO
    out = jnp.where(quarter == 3, u[:half], lane_roll(v[:half], -HALO))
    out = jnp.where(quarter == 1, lane_roll(u[half:], -2 * HALO), out)
    return jnp.where(quarter == 0, lane_roll(v[half:], -3 * HALO), out)


def unpack(right, left):
    low = iota(right.shape, 1) < LANES // 2
    u = jnp.concatenate(
        [jnp.where(low, right, left), jnp.where(low, lane_roll(right, -2 * HALO), lane_roll(left, 2 * HALO))], axis=0
    )
    v = jnp.concatenate(
        [
            jnp.where(low, lane_roll(right, -HALO), lane_roll(left, HALO)),
            jnp.where(low, lane_roll(right, -3 * HALO), lane_roll(left, 3 * HALO)),
        ],
        axis=0,
    )
    return u, v


def stencil(state, now, rate, base, rows):
    lane = iota((rows, LANES), 1)
    first = lane == 0
    last = lane == LANES - 1
    centers = []
    sums = []
    for species in range(2):
        mid = [state[now, species, tile, pl.ds(base, rows), :] for tile in range(3)]
        east = [lane_roll(value, -1) for value in mid]
        west = [lane_roll(value, 1) for value in mid]
        total = []
        for tile in range(3):
            north = state[now, species, tile, pl.ds(base - 1, rows), :]
            south = state[now, species, tile, pl.ds(base + 1, rows), :]
            right = jnp.where(last, east[(tile + 1) % 3], east[tile])
            left = jnp.where(first, west[(tile + 2) % 3], west[tile])
            total.append((north + south) + (right + left))
        centers.append(mid)
        sums.append(total)
    keep_u = 0.2 - rate
    keep_v = 0.54 - rate
    for tile in range(3):
        u = centers[0][tile]
        v = centers[1][tile]
        react = u * v * v
        state[now + 1, 0, tile, pl.ds(base, rows), :] = keep_u * u + 0.2 * sums[0][tile] + (rate - react)
        state[now + 1, 1, tile, pl.ds(base, rows), :] = keep_v * v + 0.1 * sums[1][tile] + react


def simulate_kernel(
    ramp, mask_hbm, noise_hbm, cent, gram_out,
    noise, mask, state, side_out, side_in, corner_out, corner_in, gram8, planes, lines,
    in_sem, halo_send, halo_recv, plane_send, plane_recv, line_send, line_recv,
):
    gy = lax.axis_index("gy")
    gx = lax.axis_index("gx")
    z = gx // NX
    x = gx % NX
    up = (gy + NGY - 1) % NGY
    down = (gy + 1) % NGY
    west = (gx + NX * NZ - 1) % (NX * NZ)
    east = (gx + 1) % (NX * NZ)
    me = gy * NX + x

    loads = [
        pltpu.make_async_copy(noise_hbm, noise, in_sem.at[0]),
        pltpu.make_async_copy(mask_hbm, mask, in_sem.at[1]),
    ]
    for load in loads:
        load.start()

    barrier = pltpu.get_barrier_semaphore()
    around = [(up, gx), (down, gx), (gy, west), (gy, east), (up, west), (up, east), (down, west), (down, east)]
    for device in around:
        pl.semaphore_signal(barrier, inc=1, device_id=device, device_id_type=MESH)

    def plane_peer(step):
        peer = (me + step) % PLANE
        return (peer // NX, z * NX + peer % NX)

    def line_peer(step):
        return (gy, ((z + step) % NZ) * NX + x)

    def greet_plane(step, carry):
        pl.semaphore_signal(barrier, inc=1, device_id=plane_peer(step), device_id_type=MESH)
        return carry

    def greet_line(step, carry):
        pl.semaphore_signal(barrier, inc=1, device_id=line_peer(step), device_id_type=MESH)
        return carry

    lax.fori_loop(1, PLANE, greet_plane, 0)
    lax.fori_loop(1, NZ, greet_line, 0)

    for load in loads:
        load.wait()
    row_pos = (gy * ROWS + iota((ROWS, LANES), 0)).astype(F32)
    amplitude = 0.1 * (0.5 + 1.5 * (row_pos + 0.5) / float(ROWS * NGY))
    for tile in range(2):
        lanes = pl.ds(tile * LANES, LANES)
        seeded = mask[:, lanes].astype(F32)
        state[0, 0, tile, pl.ds(TOP, ROWS), :] = 1.0 - 0.5 * seeded + amplitude * noise[0, :, lanes]
        state[0, 1, tile, pl.ds(TOP, ROWS), :] = 0.25 * seeded + amplitude * noise[1, :, lanes]
    inner = pl.ds(TOP, ROWS)
    high_rows = pl.ds(TOP, HALO)
    low_rows = pl.ds(BOTTOM - HALO, HALO)
    side_out[0] = pack_first(state[0, 0, 0, inner, :], state[0, 1, 0, inner, :])
    side_out[1] = pack_last(state[0, 0, 1, inner, :], state[0, 1, 1, inner, :])
    corner_out[0] = pack_first(state[0, 0, 0, high_rows, :], state[0, 1, 0, high_rows, :])
    corner_out[1] = pack_last(state[0, 0, 1, high_rows, :], state[0, 1, 1, high_rows, :])
    corner_out[2] = pack_first(state[0, 0, 0, low_rows, :], state[0, 1, 0, low_rows, :])
    corner_out[3] = pack_last(state[0, 0, 1, low_rows, :], state[0, 1, 1, low_rows, :])

    pl.semaphore_wait(barrier, len(around) + PLANE - 1 + NZ - 1)

    moves = [
        (corner_out.at[0], corner_in.at[2], (up, west)),
        (corner_out.at[1], corner_in.at[3], (up, east)),
        (corner_out.at[2], corner_in.at[0], (down, west)),
        (corner_out.at[3], corner_in.at[1], (down, east)),
        (side_out.at[0], side_in.at[0], (gy, west)),
        (side_out.at[1], side_in.at[1], (gy, east)),
        (
            state.at[0, :, pl.ds(0, 2), high_rows, :],
            state.at[0, :, pl.ds(0, 2), pl.ds(BOTTOM, HALO), :],
            (up, gx),
        ),
        (
            state.at[0, :, pl.ds(0, 2), low_rows, :],
            state.at[0, :, pl.ds(0, 2), pl.ds(PAD, HALO), :],
            (down, gx),
        ),
    ]
    copies = [
        pltpu.make_async_remote_copy(
            src_ref=source, dst_ref=target, send_sem=halo_send.at[i], recv_sem=halo_recv.at[i],
            device_id=device, device_id_type=MESH,
        )
        for i, (source, target, device) in enumerate(moves)
    ]
    for copy in copies:
        copy.start()
    for copy in copies:
        copy.wait()

    for start, right, left in (
        (PAD, corner_in[0], corner_in[1]),
        (TOP, side_in[0], side_in[1]),
        (BOTTOM, corner_in[2], corner_in[3]),
    ):
        u, v = unpack(right, left)
        state[0, 0, 2, pl.ds(start, u.shape[0]), :] = u
        state[0, 1, 2, pl.ds(start, u.shape[0]), :] = v

    for segment in range(5):
        first_step = max(8 * segment - 1, 0)
        end_step = min(8 * segment + 7, SNAPS)
        first_group = 1 + segment
        pairs = 12 - segment

        def one_step(now, carry, first_group=first_group, pairs=pairs):
            rate = 0.01 + 0.008 * ramp[now].astype(F32)

            def one_pair(pair, carry):
                base = pl.multiple_of(8 * first_group + 16 * pair, 8)
                stencil(state, now, rate, base, 16)
                return carry

            return lax.fori_loop(0, pairs, one_pair, carry)

        lax.fori_loop(first_step, end_step, one_step, 0)

    gram8[...] = jnp.zeros_like(gram8)

    def center(group, carry):
        blocks = []
        for species in range(2):
            halves = []
            for tile in range(2):
                snaps = state[pl.ds(1, SNAPS), species, tile, pl.ds(pl.multiple_of(TOP + 8 * group, 8), 8), :]
                average = jnp.sum(snaps, axis=0) * (1.0 / SNAPS)
                halves.append((snaps - average[None]).reshape(8 * SNAPS, LANES))
            block = jnp.concatenate(halves, axis=1).astype(BF16)
            cent[species * (ROWS // 8) + group] = block
            blocks.append(block)
        both = jnp.concatenate(blocks, axis=1)
        gram8[...] += lax.dot_general(both, both, (((1,), (1,)), ((), ())), preferred_element_type=F32)
        return carry

    lax.fori_loop(0, ROWS // 8, center, 0)

    size = 8 * SNAPS
    same = iota((size, size), 0) % 8 == iota((size, size), 1) % 8
    gather_rows = (iota((SNAPS, size), 0) == iota((SNAPS, size), 1) // 8).astype(F32)
    gather_cols = (iota((size, LANES), 0) // 8 == iota((size, LANES), 1) % SNAPS).astype(F32)
    partial = jnp.dot(gather_rows, jnp.where(same, gram8[...], 0.0), precision=HIGHEST, preferred_element_type=F32)
    partial = jnp.dot(partial, gather_cols, precision=HIGHEST, preferred_element_type=F32)
    quarter = iota((8, LANES), 1) // SNAPS
    packed = partial[0:8]
    for part in range(1, 4):
        packed = jnp.where(quarter == part, partial[8 * part : 8 * part + 8], packed)

    planes[me] = packed

    def plane_copy(step):
        return pltpu.make_async_remote_copy(
            src_ref=planes.at[me], dst_ref=planes.at[me], send_sem=plane_send, recv_sem=plane_recv,
            device_id=plane_peer(step), device_id_type=MESH,
        )

    def send_plane(step, carry):
        plane_copy(step).start()
        return carry

    lax.fori_loop(1, PLANE, send_plane, 0)
    whole = pltpu.make_async_remote_copy(
        src_ref=planes.at[pl.ds(0, PLANE - 1)], dst_ref=planes.at[pl.ds(0, PLANE - 1)],
        send_sem=plane_send, recv_sem=plane_recv, device_id=plane_peer(1), device_id_type=MESH,
    )
    whole.wait()
    lines[z] = jnp.sum(planes[...], axis=0)

    def send_line(step, carry):
        pltpu.make_async_remote_copy(
            src_ref=lines.at[z], dst_ref=lines.at[z], send_sem=line_send, recv_sem=line_recv,
            device_id=line_peer(step), device_id_type=MESH,
        ).start()
        return carry

    lax.fori_loop(1, NZ, send_line, 0)
    whole = pltpu.make_async_remote_copy(
        src_ref=lines.at[pl.ds(0, NZ - 1)], dst_ref=lines.at[pl.ds(0, NZ - 1)],
        send_sem=line_send, recv_sem=line_recv, device_id=line_peer(1), device_id_type=MESH,
    )
    whole.wait()
    gram_out[...] = jnp.sum(lines[...], axis=0)


def simulate(ramp, seed_mask, noise):
    size = 8 * SNAPS
    return pl.pallas_call(
        simulate_kernel,
        name="simulate",
        out_shape=(
            pltpu.VMEM((TILES, size, COLS), BF16),
            jax.ShapeDtypeStruct((8, LANES), F32),
        ),
        in_specs=[
            pl.BlockSpec(memory_space=pltpu.SMEM),
            pl.BlockSpec(memory_space=pl.ANY),
            pl.BlockSpec(memory_space=pl.ANY),
        ],
        out_specs=(pl.BlockSpec(memory_space=pltpu.VMEM), pl.BlockSpec(memory_space=pltpu.VMEM)),
        scratch_shapes=[
            pltpu.VMEM((2, ROWS, COLS), F32),
            pltpu.VMEM((ROWS, COLS), jnp.int32),
            pltpu.VMEM((SNAPS + 1, 2, 3, EXT, LANES), F32),
            pltpu.VMEM((2, ROWS // 2, LANES), F32),
            pltpu.VMEM((2, ROWS // 2, LANES), F32),
            pltpu.VMEM((4, HALO // 2, LANES), F32),
            pltpu.VMEM((4, HALO // 2, LANES), F32),
            pltpu.VMEM((size, size), F32),
            pltpu.VMEM((PLANE, 8, LANES), F32),
            pltpu.VMEM((NZ, 8, LANES), F32),
            pltpu.SemaphoreType.DMA((2,)),
            pltpu.SemaphoreType.DMA((8,)),
            pltpu.SemaphoreType.DMA((8,)),
            pltpu.SemaphoreType.DMA,
            pltpu.SemaphoreType.DMA,
            pltpu.SemaphoreType.DMA,
            pltpu.SemaphoreType.DMA,
        ],
        compiler_params=pltpu.CompilerParams(
            collective_id=0, has_side_effects=True, vmem_limit_bytes=40 * 1024 * 1024
        ),
    )(ramp, seed_mask, noise)


def solve(packed):
    gram = jnp.concatenate([lane_roll(packed, -SNAPS * part) for part in range(4)], axis=0)
    row = iota((SNAPS, LANES), 0)
    lane = iota((SNAPS, LANES), 1)
    diagonal = row == lane
    trace = jnp.sum(jnp.where(diagonal, gram, 0.0), axis=(0, 1), keepdims=True)
    shift = 0.01 * trace / SNAPS
    left = gram + jnp.where(diagonal, shift, 0.0)
    work = jnp.where(lane < SNAPS, left, lane_roll(gram, SNAPS))
    for k in range(SNAPS):
        pivot_row = work[k : k + 1, :]
        scaled = pivot_row / work[k : k + 1, k : k + 1]
        work = jnp.where(row == k, scaled, work - work[:, k : k + 1] * scaled)
    return lane_roll(work, -SNAPS)


def filter_kernel(cent, packed, out, matrix_out, weights):
    @pl.when(pl.program_id(0) == 0)
    def _():
        matrix = solve(packed[...])
        matrix_out[...] = matrix[:, :SNAPS]
        size = 8 * SNAPS
        spread_rows = (iota((size, SNAPS), 0) // 8 == iota((size, SNAPS), 1)).astype(BF16)
        spread_cols = (iota((SNAPS, size), 0) == iota((SNAPS, size), 1) // 8).astype(BF16)
        turned = jnp.transpose(matrix)[:SNAPS, :].astype(BF16)
        wide = jnp.dot(spread_rows, turned, preferred_element_type=F32).astype(BF16)
        wide = jnp.dot(wide, spread_cols, preferred_element_type=F32)
        same = iota((size, size), 0) % 8 == iota((size, size), 1) % 8
        weights[...] = jnp.where(same, wide, 0.0).astype(BF16)

    for part in range(cent.shape[0]):
        block = jnp.dot(weights[...], cent[part], preferred_element_type=F32)
        out[:, 0, pl.ds(8 * part, 8), :] = block.reshape(SNAPS, 8, COLS)


def apply_filter(cent, packed):
    size = 8 * SNAPS
    parts = 2
    steps = TILES // parts
    per_species = steps // 2
    return pl.pallas_call(
        filter_kernel,
        name="apply_filter",
        grid=(steps,),
        out_shape=(
            jax.ShapeDtypeStruct((SNAPS, 2, ROWS, COLS), F32),
            jax.ShapeDtypeStruct((SNAPS, SNAPS), F32),
        ),
        in_specs=[
            pl.BlockSpec((parts, size, COLS), lambda i: (i, 0, 0)),
            pl.BlockSpec((8, LANES), lambda i: (0, 0)),
        ],
        out_specs=(
            pl.BlockSpec((SNAPS, 1, 8 * parts, COLS), lambda i: (0, i // per_species, i % per_species, 0)),
            pl.BlockSpec((SNAPS, SNAPS), lambda i: (0, 0)),
        ),
        scratch_shapes=[pltpu.VMEM((size, size), BF16)],
        compiler_params=pltpu.CompilerParams(vmem_limit_bytes=16 * 1024 * 1024),
    )(cent, packed)


def local(ramp, seed_mask, noise):
    cent, packed = simulate(ramp, seed_mask, noise)
    return apply_filter(cent, packed)


def solution(mesh):
    return jax.shard_map(
        local,
        mesh=mesh,
        in_specs=(P(), P("gy", "gx"), P(None, "gy", "gx")),
        out_specs=(P(None, None, "gy", "gx"), P()),
        check_vma=False,
    )
```

```python
import jax
import jax.numpy as jnp
from jax import lax
from jax.experimental import pallas as pl
from jax.experimental.pallas import tpu as pltpu
from jax.sharding import PartitionSpec as P

SNAPS = 32
ROWS = 128
COLS = 256
HALO = 32
PAD = 8
TOP = PAD + HALO
EXT = ROWS + 2 * TOP
BOTTOM = TOP + ROWS
LANES = 128
WIDE = 3 * LANES
NGY = 8
NX = 4
NZ = 8
PLANE = NGY * NX
TILES = 2 * ROWS // 8
F32 = jnp.float32
BF16 = jnp.bfloat16
MESH = pl.DeviceIdType.MESH


def iota(shape, dim):
    return lax.broadcasted_iota(jnp.int32, shape, dim)


def lane_roll(value, shift):
    return pltpu.roll(value, shift % LANES, 1)


def pack_first(u, v):
    half = u.shape[0] // 2
    quarter = iota((half, LANES), 1) // HALO
    out = jnp.where(quarter == 0, u[:half], lane_roll(v[:half], HALO))
    out = jnp.where(quarter == 2, lane_roll(u[half:], 2 * HALO), out)
    return jnp.where(quarter == 3, lane_roll(v[half:], 3 * HALO), out)


def pack_last(u, v):
    half = u.shape[0] // 2
    quarter = iota((half, LANES), 1) // HALO
    out = jnp.where(quarter == 3, u[:half], lane_roll(v[:half], -HALO))
    out = jnp.where(quarter == 1, lane_roll(u[half:], -2 * HALO), out)
    return jnp.where(quarter == 0, lane_roll(v[half:], -3 * HALO), out)


def unpack(right, left):
    low = iota(right.shape, 1) < LANES // 2
    u = jnp.concatenate(
        [jnp.where(low, right, left), jnp.where(low, lane_roll(right, -2 * HALO), lane_roll(left, 2 * HALO))], axis=0
    )
    v = jnp.concatenate(
        [
            jnp.where(low, lane_roll(right, -HALO), lane_roll(left, HALO)),
            jnp.where(low, lane_roll(right, -3 * HALO), lane_roll(left, 3 * HALO)),
        ],
        axis=0,
    )
    return u, v


def woven(index):
    return 3 * (index % LANES) + index // LANES - LANES // 2


def split(value):
    high = value.astype(BF16)
    rest = value - high.astype(F32)
    middle = rest.astype(BF16)
    low = (rest - middle.astype(F32)).astype(BF16)
    return [high, middle, low]


def select_columns(values, choice):
    rows = values.shape[0]
    out = jnp.dot(jnp.concatenate(split(values), axis=0), choice, preferred_element_type=F32)
    return (out[:rows] + out[rows : 2 * rows]) + out[2 * rows :]


def stencil(state, now, rate, base, rows):
    centers = []
    sums = []
    for species in range(2):
        mid = [state[now, species, tile, pl.ds(base, rows), :] for tile in range(3)]
        east = [mid[1], mid[2], lane_roll(mid[0], -1)]
        west = [lane_roll(mid[2], 1), mid[0], mid[1]]
        total = []
        for tile in range(3):
            north = state[now, species, tile, pl.ds(base - 1, rows), :]
            south = state[now, species, tile, pl.ds(base + 1, rows), :]
            total.append((north + south) + (east[tile] + west[tile]))
        centers.append(mid)
        sums.append(total)
    keep_u = 0.2 - rate
    keep_v = 0.54 - rate
    for tile in range(3):
        u = centers[0][tile]
        v = centers[1][tile]
        react = u * v * v
        state[now + 1, 0, tile, pl.ds(base, rows), :] = keep_u * u + 0.2 * sums[0][tile] + (rate - react)
        state[now + 1, 1, tile, pl.ds(base, rows), :] = keep_v * v + 0.1 * sums[1][tile] + react


def simulate_kernel(
    ramp, mask_hbm, noise_hbm, cent, gram_out,
    noise, mask, nat, state, woven_cent, side_out, side_in, corner_out, corner_in, own_choice, side_choice,
    back_choice, gram8, planes, lines,
    in_sem, halo_send, halo_recv, plane_send, plane_recv, line_send, line_recv,
):
    gy = lax.axis_index("gy")
    gx = lax.axis_index("gx")
    z = gx // NX
    x = gx % NX
    up = (gy + NGY - 1) % NGY
    down = (gy + 1) % NGY
    west = (gx + NX * NZ - 1) % (NX * NZ)
    east = (gx + 1) % (NX * NZ)
    me = gy * NX + x

    loads = [
        pltpu.make_async_copy(noise_hbm, noise, in_sem.at[0]),
        pltpu.make_async_copy(mask_hbm, mask, in_sem.at[1]),
    ]
    for load in loads:
        load.start()

    barrier = pltpu.get_barrier_semaphore()
    around = [(up, gx), (down, gx), (gy, west), (gy, east), (up, west), (up, east), (down, west), (down, east)]
    for device in around:
        pl.semaphore_signal(barrier, inc=1, device_id=device, device_id_type=MESH)

    def plane_peer(step):
        peer = (me + step) % PLANE
        return (peer // NX, z * NX + peer % NX)

    def line_peer(step):
        return (gy, ((z + step) % NZ) * NX + x)

    def greet_plane(step, carry):
        pl.semaphore_signal(barrier, inc=1, device_id=plane_peer(step), device_id_type=MESH)
        return carry

    def greet_line(step, carry):
        pl.semaphore_signal(barrier, inc=1, device_id=line_peer(step), device_id_type=MESH)
        return carry

    lax.fori_loop(1, PLANE, greet_plane, 0)
    lax.fori_loop(1, NZ, greet_line, 0)

    own_choice[...] = (iota((COLS, WIDE), 0) == woven(iota((COLS, WIDE), 1))).astype(BF16)
    lane = iota((LANES, WIDE), 0)
    side_column = jnp.where(lane < LANES // 2, COLS + lane, lane - LANES)
    side_choice[...] = (side_column == woven(iota((LANES, WIDE), 1))).astype(BF16)
    back_choice[...] = (woven(iota((WIDE, COLS), 0)) == iota((WIDE, COLS), 1)).astype(BF16)

    for load in loads:
        load.wait()
    row_pos = (gy * ROWS + iota((ROWS, LANES), 0)).astype(F32)
    amplitude = 0.1 * (0.5 + 1.5 * (row_pos + 0.5) / float(ROWS * NGY))
    own_rows = pl.ds(HALO, ROWS)
    for tile in range(2):
        lanes = pl.ds(tile * LANES, LANES)
        seeded = mask[:, lanes].astype(F32)
        nat[0, tile, own_rows, :] = 1.0 - 0.5 * seeded + amplitude * noise[0, :, lanes]
        nat[1, tile, own_rows, :] = 0.25 * seeded + amplitude * noise[1, :, lanes]
    high_rows = pl.ds(HALO, HALO)
    low_rows = pl.ds(ROWS, HALO)
    side_out[0] = pack_first(nat[0, 0, own_rows, :], nat[1, 0, own_rows, :])
    side_out[1] = pack_last(nat[0, 1, own_rows, :], nat[1, 1, own_rows, :])
    corner_out[0] = pack_first(nat[0, 0, high_rows, :], nat[1, 0, high_rows, :])
    corner_out[1] = pack_last(nat[0, 1, high_rows, :], nat[1, 1, high_rows, :])
    corner_out[2] = pack_first(nat[0, 0, low_rows, :], nat[1, 0, low_rows, :])
    corner_out[3] = pack_last(nat[0, 1, low_rows, :], nat[1, 1, low_rows, :])

    def natural(species, rows):
        return jnp.concatenate([nat[species, 0, rows, :], nat[species, 1, rows, :]], axis=1)

    for species in range(2):
        placed = select_columns(natural(species, own_rows), own_choice[...])
        for tile in range(3):
            state[0, species, tile, pl.ds(TOP, ROWS), :] = placed[:, LANES * tile : LANES * (tile + 1)]

    pl.semaphore_wait(barrier, len(around) + PLANE - 1 + NZ - 1)

    moves = [
        (side_out.at[0], side_in.at[0], (gy, west)),
        (side_out.at[1], side_in.at[1], (gy, east)),
        (corner_out.at[0], corner_in.at[2], (up, west)),
        (corner_out.at[1], corner_in.at[3], (up, east)),
        (corner_out.at[2], corner_in.at[0], (down, west)),
        (corner_out.at[3], corner_in.at[1], (down, east)),
        (nat.at[:, :, high_rows, :], nat.at[:, :, pl.ds(HALO + ROWS, HALO), :], (up, gx)),
        (nat.at[:, :, low_rows, :], nat.at[:, :, pl.ds(0, HALO), :], (down, gx)),
    ]
    copies = [
        pltpu.make_async_remote_copy(
            src_ref=source, dst_ref=target, send_sem=halo_send.at[i], recv_sem=halo_recv.at[i],
            device_id=device, device_id_type=MESH,
        )
        for i, (source, target, device) in enumerate(moves)
    ]
    for copy in copies:
        copy.start()
    for copy in copies:
        copy.wait()

    sides = [
        unpack(corner_in[0], corner_in[1]),
        unpack(side_in[0], side_in[1]),
        unpack(corner_in[2], corner_in[3]),
    ]
    for species in range(2):
        beside = jnp.concatenate([side[species] for side in sides], axis=0)
        beside = select_columns(beside, side_choice[...])
        edge = jnp.concatenate(
            [natural(species, pl.ds(0, HALO)), natural(species, pl.ds(HALO + ROWS, HALO))], axis=0
        )
        edge = select_columns(edge, own_choice[...])
        for tile in range(3):
            lanes = slice(LANES * tile, LANES * (tile + 1))
            state[0, species, tile, pl.ds(PAD, HALO), :] = beside[:HALO, lanes] + edge[:HALO, lanes]
            state[0, species, tile, pl.ds(TOP, ROWS), :] += beside[HALO : HALO + ROWS, lanes]
            state[0, species, tile, pl.ds(BOTTOM, HALO), :] = beside[HALO + ROWS :, lanes] + edge[HALO:, lanes]

    for segment in range(5):
        first_step = max(8 * segment - 1, 0)
        end_step = min(8 * segment + 7, SNAPS)
        first_group = 1 + segment
        pairs = 12 - segment

        def one_step(now, carry, first_group=first_group, pairs=pairs):
            rate = 0.01 + 0.008 * ramp[now].astype(F32)

            def one_pair(pair, carry):
                base = pl.multiple_of(8 * first_group + 16 * pair, 8)
                stencil(state, now, rate, base, 16)
                return carry

            return lax.fori_loop(0, pairs, one_pair, carry, unroll=True)

        lax.fori_loop(first_step, end_step, one_step, 0)

    gram8[...] = jnp.zeros_like(gram8)
    groups = 4
    column = 3 * iota((8, LANES), 1) - LANES // 2

    def center(step, carry):
        blocks = []
        for group in range(groups):
            base = pl.multiple_of(TOP + 8 * groups * step + 8 * group, 8)
            for species in range(2):
                thirds = []
                for tile in range(3):
                    inside = (column + tile >= 0) & (column + tile < COLS)
                    snaps = state[pl.ds(1, SNAPS), species, tile, pl.ds(base, 8), :]
                    average = jnp.sum(snaps, axis=0) * (1.0 / SNAPS)
                    centered = jnp.where(inside[None], snaps - average[None], 0.0)
                    thirds.append(centered.reshape(8 * SNAPS, LANES).astype(BF16))
                block = jnp.concatenate(thirds, axis=1)
                woven_cent[species * (ROWS // 8) + groups * step + group] = block
                blocks.append(block)
        both = jnp.concatenate(blocks, axis=1)
        gram8[...] += lax.dot_general(both, both, (((1,), (1,)), ((), ())), preferred_element_type=F32)
        return carry

    lax.fori_loop(0, ROWS // (8 * groups), center, 0)

    size = 8 * SNAPS
    same = iota((size, size), 0) % 8 == iota((size, size), 1) % 8
    gather_rows = (iota((SNAPS, size), 0) == iota((SNAPS, size), 1) // 8).astype(BF16)
    gather_cols = (iota((size, LANES), 0) // 8 == iota((size, LANES), 1) % SNAPS).astype(BF16)
    pieces = [
        jnp.dot(gather_rows, piece, preferred_element_type=F32) for piece in split(jnp.where(same, gram8[...], 0.0))
    ]
    partial = (pieces[0] + pieces[1]) + pieces[2]
    partial = select_columns(partial, gather_cols)
    quarter = iota((8, LANES), 1) // SNAPS
    packed = partial[0:8]
    for part in range(1, 4):
        packed = jnp.where(quarter == part, partial[8 * part : 8 * part + 8], packed)

    planes[me] = packed

    def send_plane(step, carry):
        pltpu.make_async_remote_copy(
            src_ref=planes.at[me], dst_ref=planes.at[me], send_sem=plane_send, recv_sem=plane_recv,
            device_id=plane_peer(step), device_id_type=MESH,
        ).start()
        return carry

    def unweave(part, carry):
        for k in range(4):
            tile = 4 * part + k
            cent[tile] = jnp.dot(woven_cent[tile], back_choice[...], preferred_element_type=F32).astype(BF16)
        return carry

    lax.fori_loop(1, PLANE, send_plane, 0)
    lax.fori_loop(0, TILES // 8, unweave, 0)
    whole = pltpu.make_async_remote_copy(
        src_ref=planes.at[pl.ds(0, PLANE - 1)], dst_ref=planes.at[pl.ds(0, PLANE - 1)],
        send_sem=plane_send, recv_sem=plane_recv, device_id=plane_peer(1), device_id_type=MESH,
    )
    whole.wait()
    lines[z] = jnp.sum(planes[...], axis=0)

    def send_line(step, carry):
        pltpu.make_async_remote_copy(
            src_ref=lines.at[z], dst_ref=lines.at[z], send_sem=line_send, recv_sem=line_recv,
            device_id=line_peer(step), device_id_type=MESH,
        ).start()
        return carry

    lax.fori_loop(1, NZ, send_line, 0)
    lax.fori_loop(TILES // 8, TILES // 4, unweave, 0)
    whole = pltpu.make_async_remote_copy(
        src_ref=lines.at[pl.ds(0, NZ - 1)], dst_ref=lines.at[pl.ds(0, NZ - 1)],
        send_sem=line_send, recv_sem=line_recv, device_id=line_peer(1), device_id_type=MESH,
    )
    whole.wait()
    gram_out[...] = jnp.sum(lines[...], axis=0)


def simulate(ramp, seed_mask, noise):
    size = 8 * SNAPS
    return pl.pallas_call(
        simulate_kernel,
        name="simulate",
        out_shape=(
            pltpu.VMEM((TILES, size, COLS), BF16),
            jax.ShapeDtypeStruct((8, LANES), F32),
        ),
        in_specs=[
            pl.BlockSpec(memory_space=pltpu.SMEM),
            pl.BlockSpec(memory_space=pltpu.HBM),
            pl.BlockSpec(memory_space=pltpu.HBM),
        ],
        out_specs=(pl.BlockSpec(memory_space=pltpu.VMEM), pl.BlockSpec(memory_space=pltpu.VMEM)),
        scratch_shapes=[
            pltpu.VMEM((2, ROWS, COLS), F32),
            pltpu.VMEM((ROWS, COLS), jnp.int32),
            pltpu.VMEM((2, 2, ROWS + 2 * HALO, LANES), F32),
            pltpu.VMEM((SNAPS + 1, 2, 3, EXT, LANES), F32),
            pltpu.VMEM((TILES, size, WIDE), BF16),
            pltpu.VMEM((2, ROWS // 2, LANES), F32),
            pltpu.VMEM((2, ROWS // 2, LANES), F32),
            pltpu.VMEM((4, HALO // 2, LANES), F32),
            pltpu.VMEM((4, HALO // 2, LANES), F32),
            pltpu.VMEM((COLS, WIDE), BF16),
            pltpu.VMEM((LANES, WIDE), BF16),
            pltpu.VMEM((WIDE, COLS), BF16),
            pltpu.VMEM((size, size), F32),
            pltpu.VMEM((PLANE, 8, LANES), F32),
            pltpu.VMEM((NZ, 8, LANES), F32),
            pltpu.SemaphoreType.DMA((2,)),
            pltpu.SemaphoreType.DMA((8,)),
            pltpu.SemaphoreType.DMA((8,)),
            pltpu.SemaphoreType.DMA,
            pltpu.SemaphoreType.DMA,
            pltpu.SemaphoreType.DMA,
            pltpu.SemaphoreType.DMA,
        ],
        compiler_params=pltpu.CompilerParams(
            collective_id=0, has_side_effects=True, vmem_limit_bytes=44 * 1024 * 1024
        ),
    )(ramp, seed_mask, noise)


def solve(packed):
    gram = jnp.concatenate([lane_roll(packed, -SNAPS * part) for part in range(4)], axis=0)
    row = iota((SNAPS, LANES), 0)
    lane = iota((SNAPS, LANES), 1)
    diagonal = row == lane
    trace = jnp.sum(jnp.where(diagonal, gram, 0.0), axis=(0, 1), keepdims=True)
    shift = 0.01 * trace / SNAPS
    left = gram + jnp.where(diagonal, shift, 0.0)
    work = jnp.where(lane < SNAPS, left, lane_roll(gram, SNAPS))
    for k in range(SNAPS):
        pivot_row = work[k : k + 1, :]
        scaled = pivot_row / work[k : k + 1, k : k + 1]
        work = jnp.where(row == k, scaled, work - work[:, k : k + 1] * scaled)
    return lane_roll(work, -SNAPS)


def filter_kernel(cent, packed, out, matrix_out, weights):
    @pl.when(pl.program_id(0) == 0)
    def _():
        matrix = solve(packed[...])
        matrix_out[...] = matrix[:, :SNAPS]
        size = 8 * SNAPS
        spread_rows = (iota((size, SNAPS), 0) // 8 == iota((size, SNAPS), 1)).astype(BF16)
        spread_cols = (iota((SNAPS, size), 0) == iota((SNAPS, size), 1) // 8).astype(BF16)
        turned = jnp.transpose(matrix)[:SNAPS, :].astype(BF16)
        wide = jnp.dot(spread_rows, turned, preferred_element_type=F32).astype(BF16)
        wide = jnp.dot(wide, spread_cols, preferred_element_type=F32)
        same = iota((size, size), 0) % 8 == iota((size, size), 1) % 8
        weights[...] = jnp.where(same, wide, 0.0).astype(BF16)

    for part in range(cent.shape[0]):
        block = jnp.dot(weights[...], cent[part], preferred_element_type=F32)
        out[:, 0, pl.ds(8 * part, 8), :] = block.reshape(SNAPS, 8, COLS)


def apply_filter(cent, packed):
    size = 8 * SNAPS
    parts = 8
    steps = TILES // parts
    per_species = steps // 2
    return pl.pallas_call(
        filter_kernel,
        name="apply_filter",
        grid=(steps,),
        out_shape=(
            jax.ShapeDtypeStruct((SNAPS, 2, ROWS, COLS), F32),
            jax.ShapeDtypeStruct((SNAPS, SNAPS), F32),
        ),
        in_specs=[
            pl.BlockSpec((parts, size, COLS), lambda i: (i, 0, 0)),
            pl.BlockSpec((8, LANES), lambda i: (0, 0)),
        ],
        out_specs=(
            pl.BlockSpec((SNAPS, 1, 8 * parts, COLS), lambda i: (0, i // per_species, i % per_species, 0)),
            pl.BlockSpec((SNAPS, SNAPS), lambda i: (0, 0)),
        ),
        scratch_shapes=[pltpu.VMEM((size, size), BF16)],
        compiler_params=pltpu.CompilerParams(vmem_limit_bytes=12 * 1024 * 1024),
    )(cent, packed)


def local(ramp, seed_mask, noise):
    cent, packed = simulate(ramp, seed_mask, noise)
    return apply_filter(cent, packed)


def solution(mesh):
    return jax.shard_map(
        local,
        mesh=mesh,
        in_specs=(P(), P("gy", "gx"), P(None, "gy", "gx")),
        out_specs=(P(None, None, "gy", "gx"), P()),
        check_vma=False,
    )
```

```python
import jax
import jax.numpy as jnp
from jax import lax
from jax.experimental import pallas as pl
from jax.experimental.pallas import tpu as pltpu
from jax.sharding import PartitionSpec as P

SNAPS = 32
ROWS = 128
COLS = 256
HALO = 32
PAD = 8
TOP = PAD + HALO
EXT = ROWS + 2 * TOP
BOTTOM = TOP + ROWS
LANES = 128
WIDE = 3 * LANES
NGY = 8
NX = 4
NZ = 8
PLANE = NGY * NX
TILES = 2 * ROWS // 8
F32 = jnp.float32
BF16 = jnp.bfloat16
MESH = pl.DeviceIdType.MESH


def iota(shape, dim):
    return lax.broadcasted_iota(jnp.int32, shape, dim)


def lane_roll(value, shift):
    return pltpu.roll(value, shift % LANES, 1)


def pack_first(u, v):
    half = u.shape[0] // 2
    quarter = iota((half, LANES), 1) // HALO
    out = jnp.where(quarter == 0, u[:half], lane_roll(v[:half], HALO))
    out = jnp.where(quarter == 2, lane_roll(u[half:], 2 * HALO), out)
    return jnp.where(quarter == 3, lane_roll(v[half:], 3 * HALO), out)


def pack_last(u, v):
    half = u.shape[0] // 2
    quarter = iota((half, LANES), 1) // HALO
    out = jnp.where(quarter == 3, u[:half], lane_roll(v[:half], -HALO))
    out = jnp.where(quarter == 1, lane_roll(u[half:], -2 * HALO), out)
    return jnp.where(quarter == 0, lane_roll(v[half:], -3 * HALO), out)


def unpack(right, left):
    low = iota(right.shape, 1) < LANES // 2
    u = jnp.concatenate(
        [jnp.where(low, right, left), jnp.where(low, lane_roll(right, -2 * HALO), lane_roll(left, 2 * HALO))], axis=0
    )
    v = jnp.concatenate(
        [
            jnp.where(low, lane_roll(right, -HALO), lane_roll(left, HALO)),
            jnp.where(low, lane_roll(right, -3 * HALO), lane_roll(left, 3 * HALO)),
        ],
        axis=0,
    )
    return u, v


def woven(index):
    return 3 * (index % LANES) + index // LANES - LANES // 2


def split(value):
    high = value.astype(BF16)
    rest = value - high.astype(F32)
    middle = rest.astype(BF16)
    low = (rest - middle.astype(F32)).astype(BF16)
    return [high, middle, low]


def select_columns(values, choice):
    rows = values.shape[0]
    out = jnp.dot(jnp.concatenate(split(values), axis=0), choice, preferred_element_type=F32)
    return (out[:rows] + out[rows : 2 * rows]) + out[2 * rows :]


def stencil(state, now, rate, base, rows):
    centers = []
    sums = []
    for species in range(2):
        mid = [state[now, species, tile, pl.ds(base, rows), :] for tile in range(3)]
        east = [mid[1], mid[2], lane_roll(mid[0], -1)]
        west = [lane_roll(mid[2], 1), mid[0], mid[1]]
        total = []
        for tile in range(3):
            north = state[now, species, tile, pl.ds(base - 1, rows), :]
            south = state[now, species, tile, pl.ds(base + 1, rows), :]
            total.append((north + south) + (east[tile] + west[tile]))
        centers.append(mid)
        sums.append(total)
    keep_u = 0.2 - rate
    keep_v = 0.54 - rate
    for tile in range(3):
        u = centers[0][tile]
        v = centers[1][tile]
        react = u * v * v
        state[now + 1, 0, tile, pl.ds(base, rows), :] = keep_u * u + 0.2 * sums[0][tile] + (rate - react)
        state[now + 1, 1, tile, pl.ds(base, rows), :] = keep_v * v + 0.1 * sums[1][tile] + react


def simulate_kernel(
    ramp, mask_hbm, noise_hbm, cent, gram_out,
    noise, mask, nat, state, woven_cent, side_out, side_in, corner_out, corner_in, own_choice, side_choice,
    back_choice, gram8, planes, lines,
    in_sem, halo_send, halo_recv, plane_send, plane_recv, line_send, line_recv,
):
    gy = lax.axis_index("gy")
    gx = lax.axis_index("gx")
    z = gx // NX
    x = gx % NX
    up = (gy + NGY - 1) % NGY
    down = (gy + 1) % NGY
    west = (gx + NX * NZ - 1) % (NX * NZ)
    east = (gx + 1) % (NX * NZ)
    me = gy * NX + x

    loads = [
        pltpu.make_async_copy(noise_hbm, noise, in_sem.at[0]),
        pltpu.make_async_copy(mask_hbm, mask, in_sem.at[1]),
    ]
    for load in loads:
        load.start()

    barrier = pltpu.get_barrier_semaphore()
    around = [(up, gx), (down, gx), (gy, west), (gy, east), (up, west), (up, east), (down, west), (down, east)]
    for device in around:
        pl.semaphore_signal(barrier, inc=1, device_id=device, device_id_type=MESH)

    def plane_peer(step):
        peer = (me + step) % PLANE
        return (peer // NX, z * NX + peer % NX)

    def line_peer(step):
        return (gy, ((z + step) % NZ) * NX + x)

    def greet_plane(step, carry):
        pl.semaphore_signal(barrier, inc=1, device_id=plane_peer(step), device_id_type=MESH)
        return carry

    def greet_line(step, carry):
        pl.semaphore_signal(barrier, inc=1, device_id=line_peer(step), device_id_type=MESH)
        return carry

    lax.fori_loop(1, PLANE, greet_plane, 0)
    lax.fori_loop(1, NZ, greet_line, 0)

    for load in loads:
        load.wait()
    row_pos = (gy * ROWS + iota((ROWS, LANES), 0)).astype(F32)
    amplitude = 0.1 * (0.5 + 1.5 * (row_pos + 0.5) / float(ROWS * NGY))
    own_rows = pl.ds(HALO, ROWS)
    for tile in range(2):
        lanes = pl.ds(tile * LANES, LANES)
        seeded = mask[:, lanes].astype(F32)
        nat[0, tile, own_rows, :] = 1.0 - 0.5 * seeded + amplitude * noise[0, :, lanes]
        nat[1, tile, own_rows, :] = 0.25 * seeded + amplitude * noise[1, :, lanes]
    high_rows = pl.ds(HALO, HALO)
    low_rows = pl.ds(ROWS, HALO)
    side_out[0] = pack_first(nat[0, 0, own_rows, :], nat[1, 0, own_rows, :])
    side_out[1] = pack_last(nat[0, 1, own_rows, :], nat[1, 1, own_rows, :])
    corner_out[0] = pack_first(nat[0, 0, high_rows, :], nat[1, 0, high_rows, :])
    corner_out[1] = pack_last(nat[0, 1, high_rows, :], nat[1, 1, high_rows, :])
    corner_out[2] = pack_first(nat[0, 0, low_rows, :], nat[1, 0, low_rows, :])
    corner_out[3] = pack_last(nat[0, 1, low_rows, :], nat[1, 1, low_rows, :])

    pl.semaphore_wait(barrier, len(around) + PLANE - 1 + NZ - 1)

    moves = [
        (side_out.at[0], side_in.at[0], (gy, west)),
        (side_out.at[1], side_in.at[1], (gy, east)),
        (corner_out.at[0], corner_in.at[2], (up, west)),
        (corner_out.at[1], corner_in.at[3], (up, east)),
        (corner_out.at[2], corner_in.at[0], (down, west)),
        (corner_out.at[3], corner_in.at[1], (down, east)),
        (nat.at[:, :, high_rows, :], nat.at[:, :, pl.ds(HALO + ROWS, HALO), :], (up, gx)),
        (nat.at[:, :, low_rows, :], nat.at[:, :, pl.ds(0, HALO), :], (down, gx)),
    ]
    copies = [
        pltpu.make_async_remote_copy(
            src_ref=source, dst_ref=target, send_sem=halo_send.at[i], recv_sem=halo_recv.at[i],
            device_id=device, device_id_type=MESH,
        )
        for i, (source, target, device) in enumerate(moves)
    ]
    for copy in copies:
        copy.start()

    own_choice[...] = (iota((COLS, WIDE), 0) == woven(iota((COLS, WIDE), 1))).astype(BF16)
    lane = iota((LANES, WIDE), 0)
    side_column = jnp.where(lane < LANES // 2, COLS + lane, lane - LANES)
    side_choice[...] = (side_column == woven(iota((LANES, WIDE), 1))).astype(BF16)
    back_choice[...] = (woven(iota((WIDE, COLS), 0)) == iota((WIDE, COLS), 1)).astype(BF16)

    def natural(species, rows):
        return jnp.concatenate([nat[species, 0, rows, :], nat[species, 1, rows, :]], axis=1)

    for species in range(2):
        placed = select_columns(natural(species, own_rows), own_choice[...])
        for tile in range(3):
            state[0, species, tile, pl.ds(TOP, ROWS), :] = placed[:, LANES * tile : LANES * (tile + 1)]

    for copy in copies:
        copy.wait()

    sides = [
        unpack(corner_in[0], corner_in[1]),
        unpack(side_in[0], side_in[1]),
        unpack(corner_in[2], corner_in[3]),
    ]
    for species in range(2):
        beside = jnp.concatenate([side[species] for side in sides], axis=0)
        beside = select_columns(beside, side_choice[...])
        edge = jnp.concatenate(
            [natural(species, pl.ds(0, HALO)), natural(species, pl.ds(HALO + ROWS, HALO))], axis=0
        )
        edge = select_columns(edge, own_choice[...])
        for tile in range(3):
            lanes = slice(LANES * tile, LANES * (tile + 1))
            state[0, species, tile, pl.ds(PAD, HALO), :] = beside[:HALO, lanes] + edge[:HALO, lanes]
            state[0, species, tile, pl.ds(TOP, ROWS), :] += beside[HALO : HALO + ROWS, lanes]
            state[0, species, tile, pl.ds(BOTTOM, HALO), :] = beside[HALO + ROWS :, lanes] + edge[HALO:, lanes]

    for segment in range(5):
        first_step = max(8 * segment - 1, 0)
        end_step = min(8 * segment + 7, SNAPS)
        first_group = 1 + segment
        pairs = 12 - segment

        def one_step(now, carry, first_group=first_group, pairs=pairs):
            rate = 0.01 + 0.008 * ramp[now].astype(F32)

            def one_pair(pair, carry):
                base = pl.multiple_of(8 * first_group + 16 * pair, 8)
                stencil(state, now, rate, base, 16)
                return carry

            return lax.fori_loop(0, pairs, one_pair, carry, unroll=True)

        lax.fori_loop(first_step, end_step, one_step, 0)

    gram8[...] = jnp.zeros_like(gram8)
    groups = 4
    column = 3 * iota((8, LANES), 1) - LANES // 2

    def center(step, carry):
        blocks = []
        for group in range(groups):
            base = pl.multiple_of(TOP + 8 * groups * step + 8 * group, 8)
            for species in range(2):
                thirds = []
                for tile in range(3):
                    inside = (column + tile >= 0) & (column + tile < COLS)
                    snaps = state[pl.ds(1, SNAPS), species, tile, pl.ds(base, 8), :]
                    average = jnp.sum(snaps, axis=0) * (1.0 / SNAPS)
                    centered = jnp.where(inside[None], snaps - average[None], 0.0)
                    thirds.append(centered.reshape(8 * SNAPS, LANES).astype(BF16))
                block = jnp.concatenate(thirds, axis=1)
                woven_cent[species * (ROWS // 8) + groups * step + group] = block
                blocks.append(block)
        both = jnp.concatenate(blocks, axis=1)
        gram8[...] += lax.dot_general(both, both, (((1,), (1,)), ((), ())), preferred_element_type=F32)
        return carry

    lax.fori_loop(0, ROWS // (8 * groups), center, 0)

    size = 8 * SNAPS
    same = iota((size, size), 0) % 8 == iota((size, size), 1) % 8
    gather_rows = (iota((SNAPS, size), 0) == iota((SNAPS, size), 1) // 8).astype(BF16)
    gather_cols = (iota((size, LANES), 0) // 8 == iota((size, LANES), 1) % SNAPS).astype(BF16)
    pieces = [
        jnp.dot(gather_rows, piece, preferred_element_type=F32) for piece in split(jnp.where(same, gram8[...], 0.0))
    ]
    partial = (pieces[0] + pieces[1]) + pieces[2]
    partial = select_columns(partial, gather_cols)
    quarter = iota((8, LANES), 1) // SNAPS
    packed = partial[0:8]
    for part in range(1, 4):
        packed = jnp.where(quarter == part, partial[8 * part : 8 * part + 8], packed)

    planes[me] = packed

    def send_plane(step, carry):
        pltpu.make_async_remote_copy(
            src_ref=planes.at[me], dst_ref=planes.at[me], send_sem=plane_send, recv_sem=plane_recv,
            device_id=plane_peer(step), device_id_type=MESH,
        ).start()
        return carry

    def unweave(part, carry):
        for k in range(4):
            tile = 4 * part + k
            cent[tile] = jnp.dot(woven_cent[tile], back_choice[...], preferred_element_type=F32).astype(BF16)
        return carry

    lax.fori_loop(1, PLANE, send_plane, 0)
    lax.fori_loop(0, TILES // 8, unweave, 0)
    whole = pltpu.make_async_remote_copy(
        src_ref=planes.at[pl.ds(0, PLANE - 1)], dst_ref=planes.at[pl.ds(0, PLANE - 1)],
        send_sem=plane_send, recv_sem=plane_recv, device_id=plane_peer(1), device_id_type=MESH,
    )
    whole.wait()
    lines[z] = jnp.sum(planes[...], axis=0)

    def send_line(step, carry):
        pltpu.make_async_remote_copy(
            src_ref=lines.at[z], dst_ref=lines.at[z], send_sem=line_send, recv_sem=line_recv,
            device_id=line_peer(step), device_id_type=MESH,
        ).start()
        return carry

    lax.fori_loop(1, NZ, send_line, 0)
    lax.fori_loop(TILES // 8, TILES // 4, unweave, 0)
    whole = pltpu.make_async_remote_copy(
        src_ref=lines.at[pl.ds(0, NZ - 1)], dst_ref=lines.at[pl.ds(0, NZ - 1)],
        send_sem=line_send, recv_sem=line_recv, device_id=line_peer(1), device_id_type=MESH,
    )
    whole.wait()
    gram_out[...] = jnp.sum(lines[...], axis=0)


def simulate(ramp, seed_mask, noise):
    size = 8 * SNAPS
    return pl.pallas_call(
        simulate_kernel,
        name="simulate",
        out_shape=(
            pltpu.VMEM((TILES, size, COLS), BF16),
            jax.ShapeDtypeStruct((8, LANES), F32),
        ),
        in_specs=[
            pl.BlockSpec(memory_space=pltpu.SMEM),
            pl.BlockSpec(memory_space=pltpu.HBM),
            pl.BlockSpec(memory_space=pltpu.HBM),
        ],
        out_specs=(pl.BlockSpec(memory_space=pltpu.VMEM), pl.BlockSpec(memory_space=pltpu.VMEM)),
        scratch_shapes=[
            pltpu.VMEM((2, ROWS, COLS), F32),
            pltpu.VMEM((ROWS, COLS), jnp.int32),
            pltpu.VMEM((2, 2, ROWS + 2 * HALO, LANES), F32),
            pltpu.VMEM((SNAPS + 1, 2, 3, EXT, LANES), F32),
            pltpu.VMEM((TILES, size, WIDE), BF16),
            pltpu.VMEM((2, ROWS // 2, LANES), F32),
            pltpu.VMEM((2, ROWS // 2, LANES), F32),
            pltpu.VMEM((4, HALO // 2, LANES), F32),
            pltpu.VMEM((4, HALO // 2, LANES), F32),
            pltpu.VMEM((COLS, WIDE), BF16),
            pltpu.VMEM((LANES, WIDE), BF16),
            pltpu.VMEM((WIDE, COLS), BF16),
            pltpu.VMEM((size, size), F32),
            pltpu.VMEM((PLANE, 8, LANES), F32),
            pltpu.VMEM((NZ, 8, LANES), F32),
            pltpu.SemaphoreType.DMA((2,)),
            pltpu.SemaphoreType.DMA((8,)),
            pltpu.SemaphoreType.DMA((8,)),
            pltpu.SemaphoreType.DMA,
            pltpu.SemaphoreType.DMA,
            pltpu.SemaphoreType.DMA,
            pltpu.SemaphoreType.DMA,
        ],
        compiler_params=pltpu.CompilerParams(
            collective_id=0, has_side_effects=True, vmem_limit_bytes=44 * 1024 * 1024
        ),
    )(ramp, seed_mask, noise)


def solve(packed):
    gram = jnp.concatenate([lane_roll(packed, -SNAPS * part) for part in range(4)], axis=0)
    row = iota((SNAPS, LANES), 0)
    lane = iota((SNAPS, LANES), 1)
    diagonal = row == lane
    trace = jnp.sum(jnp.where(diagonal, gram, 0.0), axis=(0, 1), keepdims=True)
    shift = 0.01 * trace / SNAPS
    left = gram + jnp.where(diagonal, shift, 0.0)
    work = jnp.where(lane < SNAPS, left, lane_roll(gram, SNAPS))
    size = 8
    for k in range(0, SNAPS, size):
        columns = [jnp.broadcast_to(work[:, k + j : k + j + 1], work.shape) for j in range(size)]
        rows = [work[k + j : k + j + 1, :] for j in range(size)]
        block = [[columns[j][k + i : k + i + 1, :] for j in range(size)] for i in range(size)]
        for j in range(size):
            inverse = 1.0 / block[j][j]
            rows[j] = rows[j] * inverse
            for m in range(j + 1, size):
                block[j][m] = block[j][m] * inverse
            for i in range(size):
                if i != j:
                    factor = block[i][j]
                    rows[i] = rows[i] - factor * rows[j]
                    for m in range(j + 1, size):
                        block[i][m] = block[i][m] - factor * block[j][m]
        for j in range(size):
            work = work - columns[j] * rows[j]
        for j in range(size):
            work = jnp.where(row == k + j, rows[j], work)
    return lane_roll(work, -SNAPS)


def filter_kernel(cent, packed, out, matrix_out, stage, sem):
    matrix = solve(packed[...])
    matrix_out[...] = matrix[:, :SNAPS]
    size = 8 * SNAPS
    spread_rows = (iota((size, SNAPS), 0) // 8 == iota((size, SNAPS), 1)).astype(BF16)
    spread_cols = (iota((SNAPS, size), 0) == iota((SNAPS, size), 1) // 8).astype(BF16)
    turned = jnp.transpose(matrix)[:SNAPS, :].astype(BF16)
    wide = jnp.dot(spread_rows, turned, preferred_element_type=F32).astype(BF16)
    wide = jnp.dot(wide, spread_cols, preferred_element_type=F32)
    same = iota((size, size), 0) % 8 == iota((size, size), 1) % 8
    weights = jnp.where(same, wide, 0.0).astype(BF16)

    parts = 2
    copies = []
    for chunk in range(TILES // parts):
        first = chunk * parts
        species = first // (ROWS // 8)
        base = 8 * (first % (ROWS // 8))
        for part in range(parts):
            block = jnp.dot(weights, cent[first + part], preferred_element_type=F32)
            stage[:, species, pl.ds(base + 8 * part, 8), :] = block.reshape(SNAPS, 8, COLS)
        rows = pl.ds(base, 8 * parts)
        copy = pltpu.make_async_copy(stage.at[:, species, rows, :], out.at[:, species, rows, :], sem.at[chunk])
        copy.start()
        copies.append(copy)
    for copy in copies:
        copy.wait()


def apply_filter(cent, packed):
    shape = (SNAPS, 2, ROWS, COLS)
    return pl.pallas_call(
        filter_kernel,
        name="apply_filter",
        out_shape=(jax.ShapeDtypeStruct(shape, F32), jax.ShapeDtypeStruct((SNAPS, SNAPS), F32)),
        in_specs=[pl.BlockSpec(memory_space=pltpu.VMEM), pl.BlockSpec(memory_space=pltpu.VMEM)],
        out_specs=(pl.BlockSpec(memory_space=pltpu.HBM), pl.BlockSpec(memory_space=pltpu.VMEM)),
        scratch_shapes=[pltpu.VMEM(shape, F32), pltpu.SemaphoreType.DMA((TILES // 2,))],
        compiler_params=pltpu.CompilerParams(vmem_limit_bytes=24 * 1024 * 1024),
    )(cent, packed)


def local(ramp, seed_mask, noise):
    ramp, seed_mask, noise = [
        pltpu.with_memory_space_constraint(value, pltpu.HBM) for value in (ramp, seed_mask, noise)
    ]
    cent, packed = simulate(ramp, seed_mask, noise)
    return apply_filter(cent, packed)


def solution(mesh):
    return jax.shard_map(
        local,
        mesh=mesh,
        in_specs=(P(), P("gy", "gx"), P(None, "gy", "gx")),
        out_specs=(P(None, None, "gy", "gx"), P()),
        check_vma=False,
    )
```
